32 devices in a mesh: row: 8 (over z, x), col: 2 (over core), rank: 2 (over y).
Axes of the slice: x: 2, y: 2, z: 4, core: 2. Of those that a mesh axis runs over, the one named last changes fastest.
Arguments:
- tensor: bfloat16 [64, 2048, 2048], P(None, 'row', 'col'), may hold values from -6 to 6
- aux_factor: bfloat16 [64, 256], P(None, 'rank'), may hold values from -0.75 to 0.75
- row_factor: bfloat16 [2048, 256], P(('row', 'col'), 'rank'), may hold values from -0.125 to 0.125
- col_factor: bfloat16 [2048, 256], P(('col', 'row'), 'rank'), may hold values from -0.125 to 0.125
Outputs:
- row_result: float32 [2048, 256], P(('row', 'col'), 'rank')
- aux_result: float32 [64, 256], P('row', 'rank')
The draws below stay inside these ranges and needn't reach their ends.
All inputs are finite; a program needn't handle non-finite values.
Results may differ from the reference program's by a relative error of at most 0.0003.
Values may be sent and summed in bfloat16 or wider, within the bound.
A program may use at most 128 MiB of HBM per device.

```python
import jax
import jax.numpy as jnp
from jax import lax

AUX = 64
ORB_ROW = 2048
ORB_COL = 2048
RANK = 256


def block_levels(key, shape, split, smallest, top_value):
    def one(position, blocks):
        steps = jax.random.uniform(jax.random.fold_in(jax.random.fold_in(key, 6), position), (blocks,), jnp.float32, smallest / len(split), top_value / len(split))
        return jnp.repeat(jnp.exp(steps), shape[position] // blocks).reshape((-1,) + (1,) * (len(shape) - position - 1))

    gain = one(*split[0])
    for cut in split[1:]:
        gain = gain * one(*cut)
    return gain


def gaussian(stream_key, dims, width, bound, cuts=(), held_as=jnp.bfloat16):
    entries = width * jax.random.normal(stream_key, dims, jnp.float32)
    if cuts:
        entries = entries * block_levels(stream_key, dims, cuts, -0.22, 0.18)
    return jnp.clip(entries, -bound, bound).astype(held_as)


def setup_inputs(seed: int = 0) -> dict:
    arg_keys = jax.random.split(jax.random.key(seed), 5)
    return {
        "tensor": gaussian(arg_keys[0], (AUX, ORB_ROW, ORB_COL), 1.0, 6.0, ((1, 8), (2, 2))),
        "aux_factor": gaussian(arg_keys[1], (AUX, RANK), AUX ** -0.5, 0.75, ((1, 2),)),
        "row_factor": gaussian(arg_keys[2], (ORB_ROW, RANK), ORB_ROW ** -0.5, 0.125, ((0, 16), (1, 2))),
        "col_factor": gaussian(arg_keys[3], (ORB_COL, RANK), ORB_COL ** -0.5, 0.125, ((0, 16), (1, 2))),
    }


def reference(tensor, aux_factor, row_factor, col_factor):
    columns = col_factor.astype(jnp.float32)
    row_panel = row_factor.astype(jnp.float32)
    aux_panel = aux_factor.astype(jnp.float32)
    row_total = jnp.zeros((ORB_ROW, RANK), jnp.float32)
    pieces = []
    for start in range(0, AUX, 8):
        slab = tensor[start:start + 8].astype(jnp.float32)
        product = jnp.dot(slab.reshape(8 * ORB_ROW, ORB_COL), columns, precision=lax.Precision.HIGHEST).reshape(8, ORB_ROW, RANK)
        row_total = row_total + jnp.sum(product * aux_panel[start:start + 8][:, None, :], axis=0)
        pieces.append(jnp.sum(product * row_panel[None, :, :], axis=1))
    return row_total, jnp.concatenate(pieces, axis=0)
```

```python
import functools

import jax
import jax.numpy as jnp
from jax import lax
from jax.experimental import pallas as pl
from jax.experimental.pallas import tpu as pltpu
from jax.sharding import PartitionSpec as P

MESH = pl.DeviceIdType.MESH
f32 = jnp.float32
scope = jax.named_scope


def kernel(R, C, Y, G, tensor, aux, rowf, colf, row_out, aux_out,
           tbuf0, tbuf1, tbuf2, colbuf, rowsrc, rowbuf, auxbuf, row_panel, aux_panel, row_acc, aux_acc, row_in, aux_in,
           t_sem, l_sem, c_send, z_recv, plane_recv, r_send, r_recv, x_send, x_recv, a_send, a_recv, p_send, p_recv):
    r = lax.axis_index("row")
    c = lax.axis_index("col")
    y = lax.axis_index("rank")
    A, I, J = tensor.shape
    jb, N = colf.shape
    ib = rowf.shape[0]
    ac = A // R
    H = R // 2
    ZH = H // 2
    half = r // H
    local = lax.rem(r, H)
    zl = local // 2
    x = lax.rem(local, 2)
    home = c == y

    def at(row, col, rank):
        return {"row": row, "col": col, "rank": rank}

    def signal(where):
        pl.semaphore_signal(barrier, inc=1, device_id=where, device_id_type=MESH)

    def settle(ref, sem):
        pltpu.make_async_copy(ref, ref, sem).wait()

    def remote(src, dst, send_sem, recv_sem, where):
        return pltpu.make_async_remote_copy(
            src_ref=src, dst_ref=dst, send_sem=send_sem, recv_sem=recv_sem, device_id=where, device_id_type=MESH)

    def slot(row, rank):
        return rank * R + row

    z = r // 2
    beside = half * ZH + lax.rem(zl + 1, ZH)
    nearer = (1 - half) * ZH + half * (ZH - 1)
    farther = (1 - half) * ZH + (1 - half) * (ZH - 1)
    columns = [(beside * 2 + x, 1), (nearer * 2 + x, 2), (farther * 2 + x, 2)]
    plane = [(z * 2 + 1 - x, 1 - y), (z * 2 + 1 - x, y), (r, 1 - y)]

    barrier = pltpu.get_barrier_semaphore()
    for row, _ in columns[::-1]:
        signal(at(row, c, y))
    for row, rank in plane:
        signal(at(row, c, rank))
    signal(at(r, 1 - c, 1 - y))
    signal(at(r, 1 - c, y))

    own_col = pltpu.make_async_copy(colf, colbuf.at[slot(r, y)], l_sem.at[0])
    own_row = pltpu.make_async_copy(rowf, rowsrc, l_sem.at[1])
    own_aux = pltpu.make_async_copy(aux, auxbuf.at[y], l_sem.at[2])
    own_col.start()
    own_row.start()
    own_aux.start()

    def order(s):
        t = s - H
        far = (1 - half) * (R - 1 - s) + half * s
        near = half * H + lax.rem(zl + 1 + lax.div(t, 2), ZH) * 2 + lax.rem(x + 1 + t, 2)
        return jnp.where(s < H, far, near)

    starts = [z * 2, beside * 2, (1 - half) * H]
    buffers = [tbuf0, tbuf1, tbuf2]
    def fetch(p):
        width = buffers[p].shape[-1]
        for s in range(R):
            pltpu.make_async_copy(
                tensor.at[pl.ds(order(s) * ac, ac), pl.ds(pl.multiple_of(y * ib, ib), ib),
                          pl.ds(pl.multiple_of(starts[p] * jb, jb), width)],
                buffers[p].at[s], t_sem.at[p]).start()

    for p in range(3):
        fetch(p)

    def to_plane(row, kind):
        ref = colbuf.at[slot(row, y)]
        for there, rank in plane:
            remote(ref, ref, c_send, plane_recv.at[kind], at(there, c, rank)).start()

    def row_copy(e):
        return remote(rowsrc, rowbuf.at[y], r_send.at[e], r_recv.at[y], at(r, e, c))

    swap = remote(auxbuf.at[y], auxbuf.at[y], x_send, x_recv, at(r, c, 1 - y))

    def small():
        swap.start()
        row_copy(1 - c).start()

        @pl.when(jnp.logical_not(home))
        def _():
            row_copy(c).start()

    with scope("ownwait"):
        own_col.wait()
        own_row.wait()
        own_aux.wait()
    with scope("barwait"):
        pl.semaphore_wait(barrier, 8)
    def along():
        ref = colbuf.at[slot(r, y)]
        for row, _ in columns:
            remote(ref, ref, c_send, z_recv.at[z], at(row, c, y)).start()

    small()
    along()
    to_plane(r, 0)

    @pl.when(home)
    def _():
        rowbuf[y] = rowsrc[...]

    row_acc[...] = jnp.zeros_like(row_acc)
    aux_acc[...] = jnp.zeros_like(aux_acc)
    def relay(which):
        for row, kind in which:
            with scope("zwait%d" % kind):
                settle(colbuf.at[slot(row, y)], z_recv.at[row // 2])
            to_plane(row, kind)

    relay(columns[:1])
    with scope("rowwait"):
        settle(auxbuf.at[1 - y], x_recv)
        settle(rowbuf.at[1 - y], r_recv.at[1 - y])

        @pl.when(jnp.logical_not(home))
        def _():
            settle(rowbuf.at[y], r_recv.at[y])

    for s in range(Y):
        row_panel[:, s * N:(s + 1) * N] = rowbuf[s].astype(f32)
        aux_panel[:, :, s * N:(s + 1) * N] = auxbuf[s].astype(f32).reshape(R, ac, N)

    def block(p, s):
        buffer = buffers[p]
        width = buffer.shape[-1]
        weights = jnp.concatenate(
            [colbuf[pl.ds(slot(starts[p], q), width // jb)].reshape(width, N) for q in range(Y)], axis=1)
        inner = jnp.dot(buffer[pl.ds(s * G, G)].reshape(G * ac * ib, width), weights, preferred_element_type=f32)
        inner = inner.reshape(G * ac, ib, Y * N)
        scale = jnp.concatenate([aux_panel[order(s * G + g)] for g in range(G)], axis=0)
        rows = jnp.sum(inner * scale[:, None, :], axis=0)
        auxs = jnp.sum(inner * row_panel[...][None], axis=1)
        for q in range(Y):
            row_acc[q] += rows[:, q * N:(q + 1) * N]
            aux_acc[pl.ds(s * G, G), q] += auxs[:, q * N:(q + 1) * N].reshape(G, ac, N)

    def place(row, col, rank):
        return (row * C + col) * Y + rank

    def aux_copy(s, e, q):
        return remote(aux_acc.at[s, q], aux_in.at[place(r, c, y)], a_send, a_recv, at(order(s), e, q))

    def step(p, s):
        block(p, s)
        if p == 2:
            for g in range(G):
                for e in range(C):
                    for q in range(Y):
                        aux_copy(s * G + g, e, q).start()
        return 0

    for p in range(3):
        with scope("wait%d" % p):
            settle(colbuf.at[pl.ds(0, 3 * max(p, 1))], plane_recv.at[p])
        with scope("load%d" % p):
            settle(buffers[p], t_sem.at[p])
        with scope("pass%d" % p):
            if p == 0:
                lax.fori_loop(0, 1, lambda s, _: step(p, s), 0)
                relay(columns[1:])
                lax.fori_loop(1, R // G, lambda s, _: step(p, s), 0)
            else:
                lax.fori_loop(0, R // G - (p == 2), lambda s, _: step(p, s), 0)
    with scope("last"):
        block(2, R // G - 1)

    def part_copy(q):
        return remote(row_acc.at[q], row_in.at[c], p_send.at[q], p_recv.at[c], at(r, y, q))

    part_copy(1 - y).start()

    @pl.when(home)
    def _():
        row_in[c] = row_acc[y]

    @pl.when(jnp.logical_not(home))
    def _():
        part_copy(y).start()

    for s in range(R - G, R - 1):
        for e in range(C):
            for q in range(Y):
                aux_copy(s, e, q).start()
    for e, q in [(1 - c, 1 - y), (c, 1 - y), (1 - c, y)]:
        aux_copy(R - 1, e, q).start()
    pltpu.make_async_copy(aux_acc.at[R - 1, y], aux_in.at[place(r, c, y)], a_recv).start()
    with scope("partwait"):
        settle(row_in.at[1 - c], p_recv.at[1 - c])

        @pl.when(jnp.logical_not(home))
        def _():
            settle(row_in.at[c], p_recv.at[c])

    row_out[...] = row_in[0] + row_in[1]
    with scope("auxwait"):
        settle(aux_in, a_recv)
    aux_out[...] = jnp.sum(aux_in[...], axis=0)

    with scope("sendwait"):
        settle(colbuf.at[pl.ds(0, Y * R - 1)], c_send)
        settle(auxbuf.at[y], x_send)
        settle(rowsrc, r_send.at[1 - c])
        settle(row_in.at[0], p_send.at[1 - y])

        @pl.when(jnp.logical_not(home))
        def _():
            settle(rowsrc, r_send.at[c])
            settle(row_in.at[0], p_send.at[y])

        settle(aux_in.at[pl.ds(0, R * C * Y - 1)], a_send)


def emit(rows, auxs, row_out, aux_out, sem):
    copies = [pltpu.make_async_copy(rows, row_out, sem.at[0]), pltpu.make_async_copy(auxs, aux_out, sem.at[1])]
    for copy in copies:
        copy.start()
    for copy in copies:
        copy.wait()


GROUP = 2


def fused(R, C, Y, tensor, aux, rowf, colf):
    A, I, J = tensor.shape
    jb, N = colf.shape
    ib = rowf.shape[0]
    ac = A // R
    bf16 = tensor.dtype
    anywhere = pl.BlockSpec(memory_space=pltpu.HBM)
    vmem = pl.BlockSpec(memory_space=pltpu.VMEM)
    dma = pltpu.SemaphoreType.DMA
    outs = pl.pallas_call(
        functools.partial(kernel, R, C, Y, GROUP),
        out_shape=(pltpu.VMEM((ib, N), f32), pltpu.VMEM((ac, N), f32)),
        in_specs=[anywhere] * 4,
        out_specs=(vmem, vmem),
        scratch_shapes=[
            pltpu.VMEM((R, ac, ib, 2 * jb), bf16),
            pltpu.VMEM((R, ac, ib, 2 * jb), bf16),
            pltpu.VMEM((R, ac, ib, J // 2), bf16),
            pltpu.VMEM((Y * R, jb, N), bf16),
            pltpu.VMEM((ib, N), bf16),
            pltpu.VMEM((Y, ib, N), bf16),
            pltpu.VMEM((Y, A, N), bf16),
            pltpu.VMEM((ib, Y * N), f32),
            pltpu.VMEM((R, ac, Y * N), f32),
            pltpu.VMEM((Y, ib, N), f32),
            pltpu.VMEM((R, Y, ac, N), f32),
            pltpu.VMEM((C, ib, N), f32),
            pltpu.VMEM((R * C * Y, ac, N), f32),
            dma((3,)), dma((3,)), dma, dma((R // 2,)), dma((3,)), dma((C,)), dma((Y,)), dma, dma, dma, dma, dma((Y,)), dma((C,)),
        ],
        compiler_params=pltpu.CompilerParams(
            collective_id=0, has_side_effects=True, vmem_limit_bytes=56 * 2**20),
    )(tensor, aux, rowf, colf)
    outs = [pltpu.with_memory_space_constraint(o, pltpu.VMEM) for o in outs]
    return pl.pallas_call(
        emit,
        out_shape=(jax.ShapeDtypeStruct((ib, N), f32), jax.ShapeDtypeStruct((ac, N), f32)),
        in_specs=[vmem] * 2,
        out_specs=(anywhere, anywhere),
        scratch_shapes=[dma((2,))],
    )(*outs)


def plain(tensor, aux_factor, row_factor, col_factor):
    row_panel = lax.all_gather(row_factor, "col", axis=0, tiled=True).astype(f32)
    columns = lax.all_gather(col_factor, "row", axis=0, tiled=True)
    A, I, J = tensor.shape
    inner = jnp.dot(tensor.reshape(A * I, J), columns, preferred_element_type=f32).reshape(A, I, -1)
    row_total = jnp.sum(inner * aux_factor.astype(f32)[:, None, :], axis=0)
    aux_total = jnp.sum(inner * row_panel[None], axis=1)
    row_result = lax.psum_scatter(row_total, "col", scatter_dimension=0, tiled=True)
    scattered = lax.psum_scatter(aux_total, "row", scatter_dimension=0, tiled=True)
    return row_result, lax.psum(scattered, "col")


def solution(mesh):
    R, C, Y = mesh.shape["row"], mesh.shape["col"], mesh.shape["rank"]

    def body(tensor, aux, rowf, colf):
        A, I, J = tensor.shape
        jb, N = colf.shape
        ib = rowf.shape[0]
        fits = (C == 2 and Y == 2 and R // 4 == 2 and R % 4 == 0 and A % (8 * R) == 0 and ib % 16 == 0 and jb % 16 == 0
                and J % 256 == 0 and N % 128 == 0 and tensor.size < 24 * 2**20)
        if fits:
            return tuple(fused(R, C, Y, tensor, aux, rowf, colf))
        return plain(tensor, aux, rowf, colf)

    return jax.shard_map(
        body,
        mesh=mesh,
        in_specs=(
            P(None, "row", "col"),
            P(None, "rank"),
            P(("row", "col"), "rank"),
            P(("col", "row"), "rank"),
        ),
        out_specs=(P(("row", "col"), "rank"), P("row", "rank")),
        check_vma=False,
    )
```

```python
import functools

import jax
import jax.numpy as jnp
from jax import lax
from jax.experimental import pallas as pl
from jax.experimental.pallas import tpu as pltpu
from jax.sharding import PartitionSpec as P

MESH = pl.DeviceIdType.MESH
f32 = jnp.float32
scope = jax.named_scope


def kernel(R, C, Y, tensor, aux, rowf, colf, row_out, aux_out,
           tbuf0, tbuf1, colbuf, rowsrc, rowbuf, auxbuf, row_panel, aux_panel, row_acc, aux_acc, row_in, aux_in,
           t_sem, l_sem, c_send, z_recv, near_recv, far_recv, r_send, r_recv, x_send, x_recv, a_send, a_recv, p_send, p_recv):
    r = lax.axis_index("row")
    c = lax.axis_index("col")
    y = lax.axis_index("rank")
    A, I, J = tensor.shape
    jb, N = colf.shape
    ib = rowf.shape[0]
    ac = A // R
    H = R // 2
    ZH = H // 2
    half = r // H
    local = lax.rem(r, H)
    zl = local // 2
    x = lax.rem(local, 2)
    home = c == y
    away = c != y

    def at(row, col, rank):
        return {"row": row, "col": col, "rank": rank}

    def signal(where):
        pl.semaphore_signal(barrier, inc=1, device_id=where, device_id_type=MESH)

    def settle(ref, sem):
        pltpu.make_async_copy(ref, ref, sem).wait()

    def remote(src, dst, send_sem, recv_sem, where):
        return pltpu.make_async_remote_copy(
            src_ref=src, dst_ref=dst, send_sem=send_sem, recv_sem=recv_sem, device_id=where, device_id_type=MESH)

    def slot(row, rank):
        return rank * R + row

    z = r // 2
    beside = half * ZH + lax.rem(zl + 1, ZH)
    nearer = (1 - half) * ZH + half * (ZH - 1)
    farther = (1 - half) * ZH + (1 - half) * (ZH - 1)
    columns = [nearer * 2 + x, farther * 2 + x]
    plane = [(z * 2 + 1 - x, 1 - y), (z * 2 + 1 - x, y), (r, 1 - y)]
    next_plane = [(beside * 2 + 1 - x, 1 - y), (beside * 2 + 1 - x, y), (beside * 2 + x, 1 - y), (beside * 2 + x, y)]

    barrier = pltpu.get_barrier_semaphore()
    for row in columns[::-1]:
        signal(at(row, c, y))
    for row, rank in next_plane + plane:
        signal(at(row, c, rank))
    signal(at(r, 1 - c, 1 - y))
    signal(at(r, 1 - c, y))

    own_col = pltpu.make_async_copy(colf, colbuf.at[slot(r, y)], l_sem.at[0])
    own_row = pltpu.make_async_copy(rowf, rowsrc, l_sem.at[1])
    own_aux = pltpu.make_async_copy(aux, auxbuf.at[y], l_sem.at[2])
    own_col.start()
    own_row.start()
    own_aux.start()

    def order(s):
        t = s - H
        far = (1 - half) * (R - 1 - s) + half * s
        near = half * H + lax.rem(zl + 1 + lax.div(t, 2), ZH) * 2 + lax.rem(x + 1 + t, 2)
        return jnp.where(s < H, far, near)

    starts = [half * H, (1 - half) * H]
    buffers = [tbuf0, tbuf1]
    def fetch(p):
        width = buffers[p].shape[-1]
        for s in range(R):
            pltpu.make_async_copy(
                tensor.at[pl.ds(order(s) * ac, ac), pl.ds(pl.multiple_of(y * ib, ib), ib),
                          pl.ds(pl.multiple_of(starts[p] * jb, jb), width)],
                buffers[p].at[s], t_sem.at[p]).start()

    for p in range(2):
        fetch(p)

    def block_copy(source, recv_sem, where):
        ref = colbuf.at[slot(source, y)]
        return remote(ref, ref, c_send, recv_sem, where)

    def row_copy(src, q, col, rank):
        return remote(src, rowbuf.at[q], r_send, r_recv.at[q], at(r, col, rank))

    def aux_swap(q, col, rank):
        return remote(auxbuf.at[q], auxbuf.at[q], x_send, x_recv, at(r, col, rank))

    def small():
        @pl.when(home)
        def _():
            aux_swap(y, c, 1 - y).start()
            row_copy(rowsrc, y, 1 - c, y).start()

        @pl.when(away)
        def _():
            row_copy(rowsrc, y, c, 1 - y).start()

    def pass_on():
        @pl.when(home)
        def _():
            rowbuf[y] = rowsrc[...]
            settle(rowbuf.at[1 - y], r_recv.at[1 - y])
            row_copy(rowbuf.at[1 - y], 1 - y, 1 - c, y).start()

        @pl.when(away)
        def _():
            settle(auxbuf.at[1 - y], x_recv)
            aux_swap(1 - y, 1 - c, y).start()

    def small_arrival():
        @pl.when(home)
        def _():
            settle(auxbuf.at[1 - y], x_recv)

        @pl.when(away)
        def _():
            for q in range(Y):
                settle(rowbuf.at[q], r_recv.at[q])

    with scope("ownwait"):
        own_col.wait()
        own_row.wait()
        own_aux.wait()
    with scope("barwait"):
        pl.semaphore_wait(barrier, 11)
    small()
    for row in columns:
        block_copy(r, z_recv.at[z], at(row, c, y)).start()
    for row, rank in next_plane + plane:
        block_copy(r, near_recv, at(row, c, rank)).start()

    row_acc[...] = jnp.zeros_like(row_acc)
    aux_acc[...] = jnp.zeros_like(aux_acc)
    def relay():
        for row in columns:
            with scope("zwait"):
                settle(colbuf.at[slot(row, y)], z_recv.at[row // 2])
            for there, rank in plane:
                block_copy(row, far_recv, at(there, c, rank)).start()

    pass_on()
    relay()
    with scope("rowwait"):
        small_arrival()

    for s in range(Y):
        row_panel[:, s * N:(s + 1) * N] = rowbuf[s].astype(f32)
        aux_panel[:, :, s * N:(s + 1) * N] = auxbuf[s].astype(f32).reshape(R, ac, N)

    def block(p, s, G, i, span):
        buffer = buffers[p]
        width = buffer.shape[-1]
        i = pl.multiple_of(i, span)
        weights = jnp.concatenate(
            [colbuf[pl.ds(slot(starts[p], q), width // jb)].reshape(width, N) for q in range(Y)], axis=1)
        tiles = buffer[pl.ds(s, G), :, pl.ds(i, span), :].reshape(G * ac * span, width)
        inner = jnp.dot(tiles, weights, preferred_element_type=f32).reshape(G * ac, span, Y * N)
        scale = jnp.concatenate([aux_panel[order(s + g)] for g in range(G)], axis=0)
        rows = jnp.sum(inner * scale[:, None, :], axis=0)
        auxs = jnp.sum(inner * row_panel[pl.ds(i, span), :][None], axis=1)
        for q in range(Y):
            row_acc[q, pl.ds(i, span), :] += rows[:, q * N:(q + 1) * N]
            aux_acc[pl.ds(s, G), q] += auxs[:, q * N:(q + 1) * N].reshape(G, ac, N)

    def place(row, col, rank):
        return (row * C + col) * Y + rank

    def aux_copy(s, e, q):
        return remote(aux_acc.at[s, q], aux_in.at[place(r, c, y)], a_send, a_recv, at(order(s), e, q))

    others = [(1 - c, 1 - y), (c, 1 - y), (1 - c, y)]

    def spread(s, G):
        for g in range(G):
            for e, q in others + [(c, y)]:
                aux_copy(s + g, e, q).start()

    def part_copy(q, i, span):
        part = pl.ds(i, span)
        return remote(row_acc.at[q, part], row_in.at[c, part], p_send.at[q], p_recv.at[c], at(r, y, q))

    def parts(i, span):
        i = pl.multiple_of(i, span)
        part_copy(1 - y, i, span).start()

        @pl.when(away)
        def _():
            part_copy(y, i, span).start()

    with scope("wait0"):
        settle(colbuf.at[pl.ds(0, 7)], near_recv)
    with scope("load0"):
        settle(tbuf0, t_sem.at[0])
    def first(s, _):
        block(0, s * G0, G0, 0, ib)
        return 0

    def second(s, _):
        block(1, s * G2, G2, 0, ib)

        @pl.when(s < R // G2 - 1)
        def _():
            spread(s * G2, G2)

        return 0

    with scope("pass0"):
        lax.fori_loop(0, R // G0, first, 0)
    with scope("wait1"):
        settle(colbuf.at[pl.ds(0, 6)], far_recv)
        settle(tbuf1, t_sem.at[1])
    with scope("pass1"):
        lax.fori_loop(0, R // G2, second, 0)
    parts(0, ib)

    spread(R - G2, G2 - 1)
    for e, q in others:
        aux_copy(R - 1, e, q).start()

    @pl.when(home)
    def _():
        row_in[c] = row_acc[y]

    pltpu.make_async_copy(aux_acc.at[R - 1, y], aux_in.at[place(r, c, y)], a_recv).start()
    with scope("partwait"):
        settle(row_in.at[1 - c], p_recv.at[1 - c])

        @pl.when(away)
        def _():
            settle(row_in.at[c], p_recv.at[c])

    row_out[...] = row_in[0] + row_in[1]
    with scope("auxwait"):
        settle(aux_in, a_recv)
    aux_out[...] = jnp.sum(aux_in[...], axis=0)

    with scope("sendwait"):
        settle(colbuf.at[pl.ds(0, Y * R - 1)], c_send)
        settle(auxbuf.at[y], x_send)
        settle(row_in.at[0], p_send.at[1 - y])

        @pl.when(away)
        def _():
            settle(rowsrc, r_send)
            settle(row_in.at[0], p_send.at[y])

        @pl.when(home)
        def _():
            settle(rowbuf, r_send)

        settle(aux_in.at[pl.ds(0, R * C * Y - 1)], a_send)


def emit(rows, auxs, row_out, aux_out, sem):
    copies = [pltpu.make_async_copy(rows, row_out, sem.at[0]), pltpu.make_async_copy(auxs, aux_out, sem.at[1])]
    for copy in copies:
        copy.start()
    for copy in copies:
        copy.wait()


G0 = 4
G2 = 4


def fused(R, C, Y, tensor, aux, rowf, colf):
    A, I, J = tensor.shape
    jb, N = colf.shape
    ib = rowf.shape[0]
    ac = A // R
    bf16 = tensor.dtype
    anywhere = pl.BlockSpec(memory_space=pltpu.HBM)
    vmem = pl.BlockSpec(memory_space=pltpu.VMEM)
    dma = pltpu.SemaphoreType.DMA
    outs = pl.pallas_call(
        functools.partial(kernel, R, C, Y),
        out_shape=(pltpu.VMEM((ib, N), f32), pltpu.VMEM((ac, N), f32)),
        in_specs=[anywhere] * 4,
        out_specs=(vmem, vmem),
        scratch_shapes=[
            pltpu.VMEM((R, ac, ib, J // 2), bf16),
            pltpu.VMEM((R, ac, ib, J // 2), bf16),
            pltpu.VMEM((Y * R, jb, N), bf16),
            pltpu.VMEM((ib, N), bf16),
            pltpu.VMEM((Y, ib, N), bf16),
            pltpu.VMEM((Y, A, N), bf16),
            pltpu.VMEM((ib, Y * N), f32),
            pltpu.VMEM((R, ac, Y * N), f32),
            pltpu.VMEM((Y, ib, N), f32),
            pltpu.VMEM((R, Y, ac, N), f32),
            pltpu.VMEM((C, ib, N), f32),
            pltpu.VMEM((R * C * Y, ac, N), f32),
            dma((2,)), dma((3,)), dma, dma((R // 2,)), dma, dma, dma, dma((Y,)), dma, dma, dma, dma, dma((Y,)), dma((C,)),
        ],
        compiler_params=pltpu.CompilerParams(
            collective_id=0, has_side_effects=True, vmem_limit_bytes=56 * 2**20),
    )(tensor, aux, rowf, colf)
    outs = [pltpu.with_memory_space_constraint(o, pltpu.VMEM) for o in outs]
    return pl.pallas_call(
        emit,
        out_shape=(jax.ShapeDtypeStruct((ib, N), f32), jax.ShapeDtypeStruct((ac, N), f32)),
        in_specs=[vmem] * 2,
        out_specs=(anywhere, anywhere),
        scratch_shapes=[dma((2,))],
    )(*outs)


def plain(tensor, aux_factor, row_factor, col_factor):
    row_panel = lax.all_gather(row_factor, "col", axis=0, tiled=True).astype(f32)
    columns = lax.all_gather(col_factor, "row", axis=0, tiled=True)
    A, I, J = tensor.shape
    inner = jnp.dot(tensor.reshape(A * I, J), columns, preferred_element_type=f32).reshape(A, I, -1)
    row_total = jnp.sum(inner * aux_factor.astype(f32)[:, None, :], axis=0)
    aux_total = jnp.sum(inner * row_panel[None], axis=1)
    row_result = lax.psum_scatter(row_total, "col", scatter_dimension=0, tiled=True)
    scattered = lax.psum_scatter(aux_total, "row", scatter_dimension=0, tiled=True)
    return row_result, lax.psum(scattered, "col")


def solution(mesh):
    R, C, Y = mesh.shape["row"], mesh.shape["col"], mesh.shape["rank"]

    def body(tensor, aux, rowf, colf):
        A, I, J = tensor.shape
        jb, N = colf.shape
        ib = rowf.shape[0]
        fits = (C == 2 and Y == 2 and R // 4 == 2 and R % 4 == 0 and A % (8 * R) == 0 and ib % 16 == 0 and jb % 16 == 0
                and J % 256 == 0 and N % 128 == 0 and tensor.size < 24 * 2**20)
        if fits:
            return tuple(fused(R, C, Y, tensor, aux, rowf, colf))
        return plain(tensor, aux, rowf, colf)

    return jax.shard_map(
        body,
        mesh=mesh,
        in_specs=(
            P(None, "row", "col"),
            P(None, "rank"),
            P(("row", "col"), "rank"),
            P(("col", "row"), "rank"),
        ),
        out_specs=(P(("row", "col"), "rank"), P("row", "rank")),
        check_vma=False,
    )
```

```python
import functools

import jax
import jax.numpy as jnp
from jax import lax
from jax.experimental import pallas as pl
from jax.experimental.pallas import tpu as pltpu
from jax.sharding import PartitionSpec as P

MESH = pl.DeviceIdType.MESH
f32 = jnp.float32
scope = jax.named_scope


def kernel(R, C, Y, tensor, aux, rowf, colf, row_out, aux_out,
           tbuf0, tbuf1, tbuf2, colbuf, rowsrc, rowbuf, auxbuf, row_panel, aux_panel, row_acc, aux_acc, row_in, aux_in,
           t_sem, l_sem, c_send, z_recv, near_recv, far_recv, r_send, r_recv, x_send, x_recv, a_send, a_recv, p_send, p_recv):
    r = lax.axis_index("row")
    c = lax.axis_index("col")
    y = lax.axis_index("rank")
    A, I, J = tensor.shape
    jb, N = colf.shape
    ib = rowf.shape[0]
    ac = A // R
    H = R // 2
    ZH = H // 2
    half = r // H
    local = lax.rem(r, H)
    zl = local // 2
    x = lax.rem(local, 2)
    home = c == y
    away = c != y

    def at(row, col, rank):
        return {"row": row, "col": col, "rank": rank}

    def signal(where):
        pl.semaphore_signal(barrier, inc=1, device_id=where, device_id_type=MESH)

    def settle(ref, sem):
        pltpu.make_async_copy(ref, ref, sem).wait()

    def remote(src, dst, send_sem, recv_sem, where):
        return pltpu.make_async_remote_copy(
            src_ref=src, dst_ref=dst, send_sem=send_sem, recv_sem=recv_sem, device_id=where, device_id_type=MESH)

    def slot(row, rank):
        return rank * R + row

    z = r // 2
    beside = half * ZH + lax.rem(zl + 1, ZH)
    nearer = (1 - half) * ZH + half * (ZH - 1)
    farther = (1 - half) * ZH + (1 - half) * (ZH - 1)
    columns = [beside * 2 + x, nearer * 2 + x, farther * 2 + x]
    plane = [(z * 2 + 1 - x, 1 - y), (z * 2 + 1 - x, y), (r, 1 - y)]

    barrier = pltpu.get_barrier_semaphore()
    for row in columns[::-1]:
        signal(at(row, c, y))
    for row, rank in plane:
        signal(at(row, c, rank))
    signal(at(r, 1 - c, 1 - y))
    signal(at(r, 1 - c, y))

    own_col = pltpu.make_async_copy(colf, colbuf.at[slot(r, y)], l_sem.at[0])
    own_row = pltpu.make_async_copy(rowf, rowsrc, l_sem.at[1])
    own_aux = pltpu.make_async_copy(aux, auxbuf.at[y], l_sem.at[2])
    own_col.start()
    own_row.start()
    own_aux.start()

    def order(s):
        t = s - H
        far = (1 - half) * (R - 1 - s) + half * s
        near = half * H + lax.rem(zl + 1 + lax.div(t, 2), ZH) * 2 + lax.rem(x + 1 + t, 2)
        return jnp.where(s < H, far, near)

    starts = [z * 2, beside * 2, (1 - half) * H]
    buffers = [tbuf0, tbuf1, tbuf2]
    def fetch(p):
        width = buffers[p].shape[-1]
        for s in range(R):
            pltpu.make_async_copy(
                tensor.at[pl.ds(order(s) * ac, ac), pl.ds(pl.multiple_of(y * ib, ib), ib),
                          pl.ds(pl.multiple_of(starts[p] * jb, jb), width)],
                buffers[p].at[s], t_sem.at[p]).start()

    for p in range(3):
        fetch(p)

    def block_copy(source, recv_sem, where):
        ref = colbuf.at[slot(source, y)]
        return remote(ref, ref, c_send, recv_sem, where)

    def row_copy(src, q, col, rank):
        return remote(src, rowbuf.at[q], r_send, r_recv.at[q], at(r, col, rank))

    def aux_swap(q, col, rank):
        return remote(auxbuf.at[q], auxbuf.at[q], x_send, x_recv, at(r, col, rank))

    def small():
        @pl.when(home)
        def _():
            aux_swap(y, c, 1 - y).start()
            row_copy(rowsrc, y, 1 - c, y).start()

        @pl.when(away)
        def _():
            row_copy(rowsrc, y, c, 1 - y).start()

    def pass_on():
        @pl.when(home)
        def _():
            rowbuf[y] = rowsrc[...]
            settle(rowbuf.at[1 - y], r_recv.at[1 - y])
            row_copy(rowbuf.at[1 - y], 1 - y, 1 - c, y).start()

        @pl.when(away)
        def _():
            settle(auxbuf.at[1 - y], x_recv)
            aux_swap(1 - y, 1 - c, y).start()

    def small_arrival():
        @pl.when(home)
        def _():
            settle(auxbuf.at[1 - y], x_recv)

        @pl.when(away)
        def _():
            for q in range(Y):
                settle(rowbuf.at[q], r_recv.at[q])

    with scope("ownwait"):
        own_col.wait()
        own_row.wait()
        own_aux.wait()
    with scope("barwait"):
        pl.semaphore_wait(barrier, 8)
    small()
    def far_sends():
        for row in columns:
            block_copy(r, z_recv.at[z], at(row, c, y)).start()

    far_sends()
    for row, rank in plane:
        block_copy(r, near_recv.at[0], at(row, c, rank)).start()

    row_acc[...] = jnp.zeros_like(row_acc)
    aux_acc[...] = jnp.zeros_like(aux_acc)
    def relay(rows):
        for row in rows:
            with scope("zwait"):
                settle(colbuf.at[slot(row, y)], z_recv.at[row // 2])
            for there, rank in plane:
                block_copy(row, near_recv.at[1] if row is columns[0] else far_recv, at(there, c, rank)).start()

    relay(columns[:1])
    pass_on()
    relay(columns[1:])
    with scope("rowwait"):
        small_arrival()

    for s in range(Y):
        row_panel[:, s * N:(s + 1) * N] = rowbuf[s].astype(f32)
        aux_panel[:, :, s * N:(s + 1) * N] = auxbuf[s].astype(f32).reshape(R, ac, N)

    def block(p, s, G, i, span):
        buffer = buffers[p]
        width = buffer.shape[-1]
        i = pl.multiple_of(i, span)
        weights = jnp.concatenate(
            [colbuf[pl.ds(slot(starts[p], q), width // jb)].reshape(width, N) for q in range(Y)], axis=1)
        tiles = buffer[pl.ds(s, G), :, pl.ds(i, span), :].reshape(G * ac * span, width)
        inner = jnp.dot(tiles, weights, preferred_element_type=f32).reshape(G * ac, span, Y * N)
        scale = jnp.concatenate([aux_panel[order(s + g)] for g in range(G)], axis=0)
        scaled = inner * scale[:, None, :]
        cut = G * ac // CHAINS
        rows = sum(jnp.sum(scaled[n * cut:(n + 1) * cut], axis=0) for n in range(CHAINS))
        auxs = jnp.sum(inner * row_panel[pl.ds(i, span), :][None], axis=1)
        for q in range(Y):
            row_acc[q, pl.ds(i, span), :] += rows[:, q * N:(q + 1) * N]
            aux_acc[pl.ds(s, G), q] += auxs[:, q * N:(q + 1) * N].reshape(G, ac, N)

    def place(row, col, rank):
        return (row * C + col) * Y + rank

    def aux_copy(s, e, q):
        return remote(aux_acc.at[s, q], aux_in.at[place(r, c, y)], a_send, a_recv, at(order(s), e, q))

    others = [(1 - c, 1 - y), (c, 1 - y), (1 - c, y)]

    def spread(s, G):
        for g in range(G):
            for e, q in others + [(c, y)]:
                aux_copy(s + g, e, q).start()

    def part_copy(q, i, span):
        part = pl.ds(i, span)
        return remote(row_acc.at[q, part], row_in.at[c, part], p_send.at[q], p_recv.at[c], at(r, y, q))

    def parts(i, span):
        i = pl.multiple_of(i, span)
        part_copy(1 - y, i, span).start()

        @pl.when(away)
        def _():
            part_copy(y, i, span).start()

    def near(p, s):
        block(p, lax.div(s, SPANS) * G0, G0, lax.rem(s, SPANS) * (ib // SPANS), ib // SPANS)
        return 0

    def second(s, _):
        block(2, s * G2, G2, 0, ib)

        @pl.when(s < R // G2 - 1)
        def _():
            spread(s * G2, G2)

        return 0

    for p in range(2):
        with scope("wait%d" % p):
            settle(colbuf.at[pl.ds(0, 3)], near_recv.at[p])
            settle(buffers[p], t_sem.at[p])
        trips = R // G0 * SPANS
        with scope("pass%d" % p):
            lax.fori_loop(0, trips, lambda s, _: near(p, s), 0)
    with scope("wait2"):
        settle(colbuf.at[pl.ds(0, 6)], far_recv)
        settle(buffers[2], t_sem.at[2])
    with scope("pass2"):
        lax.fori_loop(0, R // G2, second, 0)
    parts(0, ib)

    spread(R - G2, G2 - 1)
    for e, q in others:
        aux_copy(R - 1, e, q).start()

    @pl.when(home)
    def _():
        row_in[c] = row_acc[y]

    pltpu.make_async_copy(aux_acc.at[R - 1, y], aux_in.at[place(r, c, y)], a_recv).start()
    with scope("partwait"):
        settle(row_in.at[1 - c], p_recv.at[1 - c])

        @pl.when(away)
        def _():
            settle(row_in.at[c], p_recv.at[c])

    row_out[...] = row_in[0] + row_in[1]
    with scope("auxwait"):
        settle(aux_in, a_recv)
    aux_out[...] = jnp.sum(aux_in[...], axis=0)

    with scope("sendwait"):
        settle(colbuf.at[pl.ds(0, Y * R - 1)], c_send)
        settle(auxbuf.at[y], x_send)
        settle(row_in.at[0], p_send.at[1 - y])

        @pl.when(away)
        def _():
            settle(rowsrc, r_send)
            settle(row_in.at[0], p_send.at[y])

        @pl.when(home)
        def _():
            settle(rowbuf, r_send)

        settle(aux_in.at[pl.ds(0, R * C * Y - 1)], a_send)


def emit(rows, auxs, row_out, aux_out, sem):
    copies = [pltpu.make_async_copy(rows, row_out, sem.at[0]), pltpu.make_async_copy(auxs, aux_out, sem.at[1])]
    for copy in copies:
        copy.start()
    for copy in copies:
        copy.wait()


G0 = 8
G2 = 4
SPANS = 2
CHAINS = 2


def fused(R, C, Y, tensor, aux, rowf, colf):
    A, I, J = tensor.shape
    jb, N = colf.shape
    ib = rowf.shape[0]
    ac = A // R
    bf16 = tensor.dtype
    anywhere = pl.BlockSpec(memory_space=pltpu.HBM)
    vmem = pl.BlockSpec(memory_space=pltpu.VMEM)
    dma = pltpu.SemaphoreType.DMA
    outs = pl.pallas_call(
        functools.partial(kernel, R, C, Y),
        out_shape=(pltpu.VMEM((ib, N), f32), pltpu.VMEM((ac, N), f32)),
        in_specs=[anywhere] * 4,
        out_specs=(vmem, vmem),
        scratch_shapes=[
            pltpu.VMEM((R, ac, ib, 2 * jb), bf16),
            pltpu.VMEM((R, ac, ib, 2 * jb), bf16),
            pltpu.VMEM((R, ac, ib, J // 2), bf16),
            pltpu.VMEM((Y * R, jb, N), bf16),
            pltpu.VMEM((ib, N), bf16),
            pltpu.VMEM((Y, ib, N), bf16),
            pltpu.VMEM((Y, A, N), bf16),
            pltpu.VMEM((ib, Y * N), f32),
            pltpu.VMEM((R, ac, Y * N), f32),
            pltpu.VMEM((Y, ib, N), f32),
            pltpu.VMEM((R, Y, ac, N), f32),
            pltpu.VMEM((C, ib, N), f32),
            pltpu.VMEM((R * C * Y, ac, N), f32),
            dma((3,)), dma((3,)), dma, dma((R // 2,)), dma((2,)), dma, dma, dma((Y,)), dma, dma, dma, dma, dma((Y,)), dma((C,)),
        ],
        compiler_params=pltpu.CompilerParams(
            collective_id=0, has_side_effects=True, vmem_limit_bytes=56 * 2**20),
    )(tensor, aux, rowf, colf)
    outs = [pltpu.with_memory_space_constraint(o, pltpu.VMEM) for o in outs]
    return pl.pallas_call(
        emit,
        out_shape=(jax.ShapeDtypeStruct((ib, N), f32), jax.ShapeDtypeStruct((ac, N), f32)),
        in_specs=[vmem] * 2,
        out_specs=(anywhere, anywhere),
        scratch_shapes=[dma((2,))],
    )(*outs)


def plain(tensor, aux_factor, row_factor, col_factor):
    row_panel = lax.all_gather(row_factor, "col", axis=0, tiled=True).astype(f32)
    columns = lax.all_gather(col_factor, "row", axis=0, tiled=True)
    A, I, J = tensor.shape
    inner = jnp.dot(tensor.reshape(A * I, J), columns, preferred_element_type=f32).reshape(A, I, -1)
    row_total = jnp.sum(inner * aux_factor.astype(f32)[:, None, :], axis=0)
    aux_total = jnp.sum(inner * row_panel[None], axis=1)
    row_result = lax.psum_scatter(row_total, "col", scatter_dimension=0, tiled=True)
    scattered = lax.psum_scatter(aux_total, "row", scatter_dimension=0, tiled=True)
    return row_result, lax.psum(scattered, "col")


def solution(mesh):
    R, C, Y = mesh.shape["row"], mesh.shape["col"], mesh.shape["rank"]

    def body(tensor, aux, rowf, colf):
        A, I, J = tensor.shape
        jb, N = colf.shape
        ib = rowf.shape[0]
        fits = (C == 2 and Y == 2 and R // 4 == 2 and R % 4 == 0 and A % (8 * R) == 0 and ib % 16 == 0 and jb % 16 == 0
                and J % 256 == 0 and N % 128 == 0 and tensor.size < 24 * 2**20)
        if fits:
            return tuple(fused(R, C, Y, tensor, aux, rowf, colf))
        return plain(tensor, aux, rowf, colf)

    return jax.shard_map(
        body,
        mesh=mesh,
        in_specs=(
            P(None, "row", "col"),
            P(None, "rank"),
            P(("row", "col"), "rank"),
            P(("col", "row"), "rank"),
        ),
        out_specs=(P(("row", "col"), "rank"), P("row", "rank")),
        check_vma=False,
    )
```

```python
import functools

import jax
import jax.numpy as jnp
from jax import lax
from jax.experimental import pallas as pl
from jax.experimental.pallas import tpu as pltpu
from jax.sharding import PartitionSpec as P

MESH = pl.DeviceIdType.MESH
f32 = jnp.float32
scope = jax.named_scope


def kernel(R, C, Y, tensor, aux, rowf, colf, row_out, aux_out,
           tbuf0, tbuf1, tbuf2, colbuf, rowsrc, rowbuf, auxbuf, row_panel, aux_panel, row_acc, aux_acc, row_in, aux_in,
           t_sem, l_sem, c_send, z_recv, near_recv, far_recv, r_send, r_recv, x_send, x_recv, a_send, a_recv, p_send, p_recv):
    r = lax.axis_index("row")
    c = lax.axis_index("col")
    y = lax.axis_index("rank")
    A, I, J = tensor.shape
    jb, N = colf.shape
    ib = rowf.shape[0]
    ac = A // R
    H = R // 2
    ZH = H // 2
    half = r // H
    local = lax.rem(r, H)
    zl = local // 2
    x = lax.rem(local, 2)
    home = c == y
    away = c != y

    def at(row, col, rank):
        return {"row": row, "col": col, "rank": rank}

    def signal(where):
        pl.semaphore_signal(barrier, inc=1, device_id=where, device_id_type=MESH)

    def settle(ref, sem):
        pltpu.make_async_copy(ref, ref, sem).wait()

    def remote(src, dst, send_sem, recv_sem, where):
        return pltpu.make_async_remote_copy(
            src_ref=src, dst_ref=dst, send_sem=send_sem, recv_sem=recv_sem, device_id=where, device_id_type=MESH)

    def slot(row, rank):
        return rank * R + row

    z = r // 2
    beside = half * ZH + lax.rem(zl + 1, ZH)
    nearer = (1 - half) * ZH + half * (ZH - 1)
    farther = (1 - half) * ZH + (1 - half) * (ZH - 1)
    columns = [beside * 2 + x, nearer * 2 + x, farther * 2 + x]
    plane = [(z * 2 + 1 - x, 1 - y), (z * 2 + 1 - x, y), (r, 1 - y)]

    barrier = pltpu.get_barrier_semaphore()
    for row in columns[::-1]:
        signal(at(row, c, y))
    for row, rank in plane:
        signal(at(row, c, rank))
    signal(at(r, 1 - c, 1 - y))
    signal(at(r, 1 - c, y))

    own_col = pltpu.make_async_copy(colf, colbuf.at[slot(r, y)], l_sem.at[0])
    own_row = pltpu.make_async_copy(rowf, rowsrc, l_sem.at[1])
    own_aux = pltpu.make_async_copy(aux, auxbuf.at[y], l_sem.at[2])
    own_col.start()
    own_row.start()
    own_aux.start()

    def order(s):
        t = s - H
        far = (1 - half) * (R - 1 - s) + half * s
        near = half * H + lax.rem(zl + 1 + lax.div(t, 2), ZH) * 2 + lax.rem(x + 1 + t, 2)
        return jnp.where(s < H, far, near)

    starts = [z * 2, beside * 2, (1 - half) * H]
    buffers = [tbuf0, tbuf1, tbuf2]
    def fetch(p):
        width = buffers[p].shape[-1]
        for s in range(R):
            pltpu.make_async_copy(
                tensor.at[pl.ds(order(s) * ac, ac), pl.ds(pl.multiple_of(y * ib, ib), ib),
                          pl.ds(pl.multiple_of(starts[p] * jb, jb), width)],
                buffers[p].at[s], t_sem.at[p]).start()

    for p in range(3):
        fetch(p)

    def block_copy(source, recv_sem, where):
        ref = colbuf.at[slot(source, y)]
        return remote(ref, ref, c_send, recv_sem, where)

    def row_copy(src, q, col, rank):
        return remote(src, rowbuf.at[q], r_send, r_recv.at[q], at(r, col, rank))

    def aux_swap(q, col, rank):
        return remote(auxbuf.at[q], auxbuf.at[q], x_send, x_recv, at(r, col, rank))

    def small():
        @pl.when(home)
        def _():
            aux_swap(y, c, 1 - y).start()
            row_copy(rowsrc, y, 1 - c, y).start()

        @pl.when(away)
        def _():
            row_copy(rowsrc, y, c, 1 - y).start()

    def pass_on():
        @pl.when(home)
        def _():
            rowbuf[y] = rowsrc[...]
            settle(rowbuf.at[1 - y], r_recv.at[1 - y])
            row_copy(rowbuf.at[1 - y], 1 - y, 1 - c, y).start()

        @pl.when(away)
        def _():
            settle(auxbuf.at[1 - y], x_recv)
            aux_swap(1 - y, 1 - c, y).start()

    def small_arrival():
        @pl.when(home)
        def _():
            settle(auxbuf.at[1 - y], x_recv)

        @pl.when(away)
        def _():
            for q in range(Y):
                settle(rowbuf.at[q], r_recv.at[q])

    with scope("ownwait"):
        own_col.wait()
        own_row.wait()
        own_aux.wait()
    with scope("barwait"):
        pl.semaphore_wait(barrier, 8)
    small()
    def far_sends():
        for row in columns:
            block_copy(r, z_recv.at[z], at(row, c, y)).start()

    far_sends()
    for row, rank in plane:
        block_copy(r, near_recv.at[0], at(row, c, rank)).start()

    row_acc[...] = jnp.zeros_like(row_acc)
    aux_acc[...] = jnp.zeros_like(aux_acc)
    def relay(rows):
        for row in rows:
            with scope("zwait"):
                settle(colbuf.at[slot(row, y)], z_recv.at[row // 2])
            for there, rank in plane:
                block_copy(row, near_recv.at[1] if row is columns[0] else far_recv, at(there, c, rank)).start()

    relay(columns[:1])
    pass_on()
    relay(columns[1:])
    with scope("rowwait"):
        small_arrival()

    for s in range(Y):
        row_panel[:, s * N:(s + 1) * N] = rowbuf[s].astype(f32)
        aux_panel[:, :, s * N:(s + 1) * N] = auxbuf[s].astype(f32).reshape(R, ac, N)

    def block(p, s, G, i, span):
        buffer = buffers[p]
        width = buffer.shape[-1]
        i = pl.multiple_of(i, span)
        weights = jnp.concatenate(
            [colbuf[pl.ds(slot(starts[p], q), width // jb)].reshape(width, N) for q in range(Y)], axis=1)
        tiles = buffer[pl.ds(s, G), :, pl.ds(i, span), :].reshape(G * ac * span, width)
        inner = jnp.dot(tiles, weights, preferred_element_type=f32).reshape(G * ac, span, Y * N)
        scale = jnp.concatenate([aux_panel[order(s + g)] for g in range(G)], axis=0)
        scaled = inner * scale[:, None, :]
        chains = CHAINS if p < 2 else 1
        cut = G * ac // chains
        rows = sum(jnp.sum(scaled[n * cut:(n + 1) * cut], axis=0) for n in range(chains))
        auxs = jnp.sum(inner * row_panel[pl.ds(i, span), :][None], axis=1)
        for q in range(Y):
            row_acc[q, pl.ds(i, span), :] += rows[:, q * N:(q + 1) * N]
            aux_acc[pl.ds(s, G), q] += auxs[:, q * N:(q + 1) * N].reshape(G, ac, N)

    def place(row, col, rank):
        return (row * C + col) * Y + rank

    def aux_copy(s, e, q):
        return remote(aux_acc.at[s, q], aux_in.at[place(r, c, y)], a_send, a_recv, at(order(s), e, q))

    others = [(1 - c, 1 - y), (c, 1 - y), (1 - c, y)]

    def spread(s, G):
        for g in range(G):
            for e, q in others + [(c, y)]:
                aux_copy(s + g, e, q).start()

    def part_copy(q, i, span):
        part = pl.ds(i, span)
        return remote(row_acc.at[q, part], row_in.at[c, part], p_send.at[q], p_recv.at[c], at(r, y, q))

    def parts(i, span):
        i = pl.multiple_of(i, span)
        part_copy(1 - y, i, span).start()

        @pl.when(away)
        def _():
            part_copy(y, i, span).start()

    def near(p, s):
        block(p, lax.div(s, SPANS) * G0, G0, lax.rem(s, SPANS) * (ib // SPANS), ib // SPANS)
        return 0

    def second(s, _):
        block(2, s * G2, G2, 0, ib)

        @pl.when(s < R // G2 - 1)
        def _():
            spread(s * G2, G2)

        return 0

    for p in range(2):
        with scope("wait%d" % p):
            settle(colbuf.at[pl.ds(0, 3)], near_recv.at[p])
            settle(buffers[p], t_sem.at[p])
        trips = R // G0 * SPANS
        with scope("pass%d" % p):
            lax.fori_loop(0, trips, lambda s, _: near(p, s), 0)
    with scope("wait2"):
        settle(colbuf.at[pl.ds(0, 6)], far_recv)
        settle(buffers[2], t_sem.at[2])
    with scope("pass2"):
        lax.fori_loop(0, R // G2, second, 0)

    spread(R - G2, G2 - 1)
    for e, q in others:
        aux_copy(R - 1, e, q).start()
    parts(0, ib)

    @pl.when(home)
    def _():
        row_in[c] = row_acc[y]

    pltpu.make_async_copy(aux_acc.at[R - 1, y], aux_in.at[place(r, c, y)], a_recv).start()
    with scope("partwait"):
        settle(row_in.at[1 - c], p_recv.at[1 - c])

        @pl.when(away)
        def _():
            settle(row_in.at[c], p_recv.at[c])

    row_out[...] = row_in[0] + row_in[1]
    with scope("auxwait"):
        settle(aux_in, a_recv)
    aux_out[...] = jnp.sum(aux_in[...], axis=0)

    with scope("sendwait"):
        settle(colbuf.at[pl.ds(0, Y * R - 1)], c_send)
        settle(auxbuf.at[y], x_send)
        settle(row_in.at[0], p_send.at[1 - y])

        @pl.when(away)
        def _():
            settle(rowsrc, r_send)
            settle(row_in.at[0], p_send.at[y])

        @pl.when(home)
        def _():
            settle(rowbuf, r_send)

        settle(aux_in.at[pl.ds(0, R * C * Y - 1)], a_send)


def emit(rows, auxs, row_out, aux_out, sem):
    copies = [pltpu.make_async_copy(rows, row_out, sem.at[0]), pltpu.make_async_copy(auxs, aux_out, sem.at[1])]
    for copy in copies:
        copy.start()
    for copy in copies:
        copy.wait()


G0 = 8
G2 = 4
SPANS = 2
CHAINS = 2


def fused(R, C, Y, tensor, aux, rowf, colf):
    A, I, J = tensor.shape
    jb, N = colf.shape
    ib = rowf.shape[0]
    ac = A // R
    bf16 = tensor.dtype
    anywhere = pl.BlockSpec(memory_space=pltpu.HBM)
    vmem = pl.BlockSpec(memory_space=pltpu.VMEM)
    dma = pltpu.SemaphoreType.DMA
    outs = pl.pallas_call(
        functools.partial(kernel, R, C, Y),
        out_shape=(pltpu.VMEM((ib, N), f32), pltpu.VMEM((ac, N), f32)),
        in_specs=[anywhere] * 4,
        out_specs=(vmem, vmem),
        scratch_shapes=[
            pltpu.VMEM((R, ac, ib, 2 * jb), bf16),
            pltpu.VMEM((R, ac, ib, 2 * jb), bf16),
            pltpu.VMEM((R, ac, ib, J // 2), bf16),
            pltpu.VMEM((Y * R, jb, N), bf16),
            pltpu.VMEM((ib, N), bf16),
            pltpu.VMEM((Y, ib, N), bf16),
            pltpu.VMEM((Y, A, N), bf16),
            pltpu.VMEM((ib, Y * N), f32),
            pltpu.VMEM((R, ac, Y * N), f32),
            pltpu.VMEM((Y, ib, N), f32),
            pltpu.VMEM((R, Y, ac, N), f32),
            pltpu.VMEM((C, ib, N), f32),
            pltpu.VMEM((R * C * Y, ac, N), f32),
            dma((3,)), dma((3,)), dma, dma((R // 2,)), dma((2,)), dma, dma, dma((Y,)), dma, dma, dma, dma, dma((Y,)), dma((C,)),
        ],
        compiler_params=pltpu.CompilerParams(
            collective_id=0, has_side_effects=True, vmem_limit_bytes=56 * 2**20),
    )(tensor, aux, rowf, colf)
    outs = [pltpu.with_memory_space_constraint(o, pltpu.VMEM) for o in outs]
    return pl.pallas_call(
        emit,
        out_shape=(jax.ShapeDtypeStruct((ib, N), f32), jax.ShapeDtypeStruct((ac, N), f32)),
        in_specs=[vmem] * 2,
        out_specs=(anywhere, anywhere),
        scratch_shapes=[dma((2,))],
    )(*outs)


def plain(tensor, aux_factor, row_factor, col_factor):
    row_panel = lax.all_gather(row_factor, "col", axis=0, tiled=True).astype(f32)
    columns = lax.all_gather(col_factor, "row", axis=0, tiled=True)
    A, I, J = tensor.shape
    inner = jnp.dot(tensor.reshape(A * I, J), columns, preferred_element_type=f32).reshape(A, I, -1)
    row_total = jnp.sum(inner * aux_factor.astype(f32)[:, None, :], axis=0)
    aux_total = jnp.sum(inner * row_panel[None], axis=1)
    row_result = lax.psum_scatter(row_total, "col", scatter_dimension=0, tiled=True)
    scattered = lax.psum_scatter(aux_total, "row", scatter_dimension=0, tiled=True)
    return row_result, lax.psum(scattered, "col")


def solution(mesh):
    R, C, Y = mesh.shape["row"], mesh.shape["col"], mesh.shape["rank"]

    def body(tensor, aux, rowf, colf):
        A, I, J = tensor.shape
        jb, N = colf.shape
        ib = rowf.shape[0]
        fits = (C == 2 and Y == 2 and R // 4 == 2 and R % 4 == 0 and A % (8 * R) == 0 and ib % 16 == 0 and jb % 16 == 0
                and J % 256 == 0 and N % 128 == 0 and tensor.size < 24 * 2**20)
        if fits:
            return tuple(fused(R, C, Y, tensor, aux, rowf, colf))
        return plain(tensor, aux, rowf, colf)

    return jax.shard_map(
        body,
        mesh=mesh,
        in_specs=(
            P(None, "row", "col"),
            P(None, "rank"),
            P(("row", "col"), "rank"),
            P(("col", "row"), "rank"),
        ),
        out_specs=(P(("row", "col"), "rank"), P("row", "rank")),
        check_vma=False,
    )
```
